128 devices in a mesh: outer: 8 (over z_lo, y), inner: 16 (over z_hi, x, core).
Axes of the slice: x: 4, y: 4, z: 4 (z_hi: 2, z_lo: 2; z = z_hi * 2 + z_lo), core: 2. Of those that a mesh axis runs over, the one named last changes fastest.
Arguments:
- tokens: bfloat16 [1024, 8192], P(None, 'outer'), may hold values from -60 to 60
- base_gate: bfloat16 [8192, 28672], P('outer', 'inner'), may hold values from -0.06629126 to 0.06629126
- base_up: bfloat16 [8192, 28672], P('outer', 'inner'), may hold values from -0.06629126 to 0.06629126
- adjusted_gate: bfloat16 [8192, 28672], P('outer', 'inner'), may hold values from -0.092807765 to 0.092807765
- adjusted_up: bfloat16 [8192, 28672], P('outer', 'inner'), may hold values from -0.092807765 to 0.092807765
- slab_block: int32 [16], replicated, may hold values from 0 to 15, each once
Outputs:
- correlation: float32 [1792, 28672], P('outer', 'inner')
The draws below stay inside these ranges and needn't reach their ends.
Inputs may be any that keep to these rules, and one draw needn't show every extreme that they name: `slab_block`: each block number appears once.
All inputs are finite; a program needn't handle non-finite values.
Results may differ from the reference program's by a relative error of at most 0.004.
Values may be sent and summed in bfloat16 or wider, within the bound.
No kernel may reach another device: no remote copies, remote signals or barrier semaphores. Data moves between devices by JAX's collectives and lax.ppermute only.
A program may use at most 192 MiB of HBM per device.

```python
import jax
import jax.numpy as jnp
from jax import lax

D = 8192
FF = 28672
TOKENS = 1024
SLAB = 1792
N_INNER = 16


def weight_pair(key, tag):
    inner_key = jax.random.fold_in(key, tag)
    base = jnp.clip(jax.random.normal(jax.random.fold_in(inner_key, 0), (D, FF), jnp.float32), -6.0, 6.0)
    fresh = jnp.clip(jax.random.normal(jax.random.fold_in(inner_key, 1), (D, FF), jnp.float32), -6.0, 6.0)
    scale = D ** (-0.5)
    return (base * scale, (0.8 * base + 0.6 * fresh) * scale)


def draw_base_gate(key, part):
    return weight_pair(key, 11)[0].astype(jnp.bfloat16)


def draw_adjusted_gate(key, part):
    return weight_pair(key, 11)[1].astype(jnp.bfloat16)


def draw_base_up(key, part):
    return weight_pair(key, 23)[0].astype(jnp.bfloat16)


def draw_adjusted_up(key, part):
    return weight_pair(key, 23)[1].astype(jnp.bfloat16)


def draw_tokens(key, part):
    inner_key = jax.random.fold_in(key, 37)
    ramp = jnp.arange(TOKENS, dtype=jnp.float32)[:, None] / max(TOKENS - 1, 1)
    spread = jax.random.uniform(jax.random.fold_in(inner_key, 0), (TOKENS, 1), jnp.float32)
    row_scale = jnp.exp(jnp.log(3.0) * ramp + jnp.log(10.0 / 3.0) * spread)
    values = jnp.clip(jax.random.normal(jax.random.fold_in(inner_key, 1), (TOKENS, D), jnp.float32), -6.0, 6.0)
    return (values * row_scale).astype(jnp.bfloat16)


def setup_inputs(seed: int = 0) -> dict:
    key_of = jax.random.split(jax.random.key(seed), 7)
    return {
        "tokens": draw_tokens(jax.random.fold_in(key_of[6], 71), 0),
        "base_gate": draw_base_gate(jax.random.fold_in(key_of[6], 71), 0),
        "base_up": draw_base_up(jax.random.fold_in(key_of[6], 71), 0),
        "adjusted_gate": draw_adjusted_gate(jax.random.fold_in(key_of[6], 71), 0),
        "adjusted_up": draw_adjusted_up(jax.random.fold_in(key_of[6], 71), 0),
        "slab_block": jax.random.permutation(key_of[5], N_INNER).astype(jnp.int32),
    }


def scores(tokens, gate_weight, up_weight):
    gate = jnp.dot(tokens, gate_weight, preferred_element_type=jnp.float32)
    up = jnp.dot(tokens, up_weight, preferred_element_type=jnp.float32)
    hidden = jax.nn.silu(gate) * up
    mean = lax.optimization_barrier(jnp.mean(hidden, axis=0, keepdims=True))
    var = lax.optimization_barrier(jnp.mean((hidden - mean) ** 2, axis=0, keepdims=True))
    return ((hidden - mean) * lax.rsqrt(var + 1e-05)).astype(jnp.bfloat16)

def reference(tokens, base_gate, base_up, adjusted_gate, adjusted_up, slab_block):
    base_scores = scores(tokens, base_gate, base_up)
    adjusted_scores = scores(tokens, adjusted_gate, adjusted_up)
    start = (slab_block[0] * SLAB).astype(jnp.int32)
    slab = lax.dynamic_slice_in_dim(base_scores, start, SLAB, 1)
    gram = lax.dot_general(slab, adjusted_scores, (((0,), (0,)), ((), ())), preferred_element_type=jnp.float32)
    return gram / TOKENS
```

```python
import jax
import jax.numpy as jnp
from jax import lax
from jax.sharding import PartitionSpec as P

Y, Z, X = 4, 2, 4
BF = jnp.bfloat16
F32 = jnp.float32


def along_y(k):
    return [(z * Y + y, z * Y + (y + k) % Y) for z in range(Z) for y in range(Y)]


def across_z():
    return [(o, o ^ Y) for o in range(Z * Y)]


def along_x(k):
    return [(h * 8 + x * 2 + c, h * 8 + (x + k) % X * 2 + c) for h in range(2) for x in range(X) for c in range(2)]


def flip(bit):
    return [(i, i ^ bit) for i in range(16)]


def outer_to(array, perm):
    return lax.ppermute(array, "outer", perm)


def inner_to(array, perm):
    return lax.ppermute(array, "inner", perm)


def pick(array, index, axis=0):
    return lax.dynamic_index_in_dim(array, index, axis, keepdims=False)


def project(weight, tokens):
    return lax.dot_general(weight, tokens, (((0,), (1,)), ((), ())), preferred_element_type=F32)


def standardized(gate, up):
    hidden = jax.nn.silu(gate) * up
    mean = jnp.mean(hidden, axis=1, keepdims=True)
    centered = hidden - mean
    var = jnp.mean(centered * centered, axis=1, keepdims=True)
    return (centered * lax.rsqrt(var + 1e-05)).astype(BF)


def summed_y_first(partial, y, z):
    total = pick(partial, y, 1)
    got = [outer_to(pick(partial, (y + k) % Y, 1).astype(BF), along_y(k)) for k in (2, 1, 3)]
    for g in got:
        total = total + g.astype(F32)
    other = outer_to(pick(total, 1 - z).astype(BF), across_z())
    return pick(total, z) + other.astype(F32)


def summed_z_first(partial, y, z):
    mine, theirs = pick(partial, z), pick(partial, 1 - z)
    total = {}
    for k in (2, 1, 3, 0):
        other = outer_to(pick(theirs, (y + k) % Y).astype(BF), across_z())
        total[k] = pick(mine, (y + k) % Y) + other.astype(F32)
    result = total[0]
    for k in (2, 1, 3):
        result = result + outer_to(total[k].astype(BF), along_y(k)).astype(F32)
    return result


def gathered(score, y, z):
    rows, count = score.shape
    half = rows // 2
    low, high = score[:half], score[half:]
    full = jnp.zeros((Z * Y * rows, count), score.dtype)

    def put(full, piece, at_z, at_y, offset):
        return lax.dynamic_update_slice(full, piece, ((at_z * Y + at_y) * rows + offset, 0))

    both = jnp.stack([low, outer_to(low, across_z())])
    highs = {0: high}
    for k in (2, 1, 3):
        highs[k] = outer_to(high, along_y(k))
    lows = {0: both}
    for k in (2, 1, 3):
        lows[k] = outer_to(both, along_y(k))
    for k in (0, 1, 3, 2):
        at = (y - k) % Y
        full = put(full, lows[k][0], z, at, 0)
        full = put(full, lows[k][1], 1 - z, at, 0)
        full = put(full, highs[k], z, at, half)
        full = put(full, outer_to(highs[k], across_z()), 1 - z, at, half)
    return full


def spread(gate, up, root, h, x, c):
    root_h, root_x, root_c = root // 8, root // 2 % X, root % 2
    depth, units = gate.shape
    half = units // 2
    both = jnp.stack([gate, up])
    cut = lambda core: lax.dynamic_slice_in_dim(both, core * half, half, 2)
    other = inner_to(cut(1 - c), flip(1))
    held = jnp.where(root_c == c, cut(c), other)
    held = jnp.pad(held, ((0, 0), (0, 0), (0, 128)))
    wide = 256
    chunk = lambda k: lax.dynamic_slice_in_dim(held, (x + k) % X * wide, wide, 2)
    far = chunk(2)
    far_gate = inner_to(far[0], along_x(1))
    far_up = inner_to(far[1], along_x(3))
    right, left = chunk(1), chunk(3)
    right = jnp.stack([jnp.where(root_x == (x + 3) % X, far_gate, right[0]), right[1]])
    left = jnp.stack([left[0], jnp.where(root_x == (x + 1) % X, far_up, left[1])])
    from_left = inner_to(right, along_x(1))
    from_right = inner_to(left, along_x(3))
    away = (root_x - x) % X
    own = chunk(0)
    got_gate = jnp.where(away == 0, own[0], jnp.where(away == 1, from_right[0], from_left[0]))
    got_up = jnp.where(away == 0, own[1], jnp.where(away == 3, from_left[1], from_right[1]))
    got = jnp.stack([got_gate, got_up])
    tile = lambda which: lax.dynamic_slice_in_dim(got, which * 128, 128, 2)
    other = inner_to(tile(1 - h), flip(8))
    return jnp.where(root_h == h, tile(h), other)


def slab_moves():
    moves = []
    for i in range(16):
        h, x, c = i // 8, i // 2 % X, i % 2
        block = 2 * x + h
        if block >= 7:
            continue
        for o in range(8):
            unit = 8 * (7 * c + block) + o
            moves.append((o * 16 + i, unit // 14 * 16 + unit % 14))
    return moves


def local(tokens, base_gate, base_up, adjusted_gate, adjusted_up, slab_block):
    units = base_gate.shape[1]
    count = tokens.shape[0]
    rows = units // (Z * Y)
    outer, inner = lax.axis_index("outer"), lax.axis_index("inner")
    z, y = outer // Y, outer % Y
    h, x, c = inner // 8, inner // 2 % X, inner % 2

    weights = spread(base_gate, base_up, slab_block[0], h, x, c)

    gate = project(adjusted_gate, tokens).reshape(Z, Y, rows, count)
    gate = summed_y_first(gate, y, z)
    up = project(adjusted_up, tokens).reshape(Z, Y, rows, count)
    up = summed_z_first(up, y, z)
    adjusted = gathered(standardized(gate, up), y, z)

    partial = jnp.stack([project(weights[0], tokens), project(weights[1], tokens)])
    partial = partial.reshape(2, Z, Y, 16, count)
    total = pick(partial, y, 2)
    for k in (2, 1, 3):
        total = total + outer_to(pick(partial, (y + k) % Y, 2), along_y(k))
    total = pick(total, z, 1) + outer_to(pick(total, 1 - z, 1), across_z())
    score = standardized(total[0], total[1])
    score = lax.ppermute(score, ("outer", "inner"), slab_moves())
    slab = jnp.zeros((16, 16, count), BF)
    pair = [score, inner_to(score, flip(1))]
    pair = jnp.stack([jnp.where(c == 0, pair[0], pair[1]), jnp.where(c == 0, pair[1], pair[0])])
    other = inner_to(pair, flip(8))
    four = jnp.stack([jnp.where(h == 0, pair, other), jnp.where(h == 0, other, pair)])
    slab = jnp.zeros((X, 2, 2, 16, count), BF)
    slab = lax.dynamic_update_slice_in_dim(slab, four[None], x, 0)
    for k in (1, 3, 2):
        slab = lax.dynamic_update_slice_in_dim(slab, inner_to(four, along_x(k))[None], (x - k) % X, 0)
    slab = slab.transpose(1, 0, 2, 3, 4).reshape(256, count)[:rows]
    gram = lax.dot_general(slab, adjusted, (((1,), (1,)), ((), ())), preferred_element_type=F32)
    return gram / count


def solution(mesh):
    return jax.shard_map(
        local,
        mesh=mesh,
        in_specs=(
            P(None, "outer"),
            P("outer", "inner"),
            P("outer", "inner"),
            P("outer", "inner"),
            P("outer", "inner"),
            P(),
        ),
        out_specs=P("outer", "inner"),
        check_vma=False,
    )
```

```python
import jax
import jax.numpy as jnp
from jax import lax
from jax.experimental import pallas as pl
from jax.experimental.pallas import tpu as pltpu
from jax.sharding import PartitionSpec as P

Y, Z, X = 4, 2, 4
TILE = 128
BLOCK = 16
BF = jnp.bfloat16
F32 = jnp.float32


def along_y(k):
    return [(z * Y + y, z * Y + (y + k) % Y) for z in range(Z) for y in range(Y)]


def across_z():
    return [(o, o ^ Y) for o in range(Z * Y)]


def along_x(k):
    return [(h * 8 + x * 2 + c, h * 8 + (x + k) % X * 2 + c) for h in range(2) for x in range(X) for c in range(2)]


def flip(bit):
    return [(i, i ^ bit) for i in range(16)]


def to_outer(array, perm):
    return lax.ppermute(array, "outer", perm)


def to_inner(array, perm):
    return lax.ppermute(array, "inner", perm)


def project(weight, tokens):
    return lax.dot_general(weight, tokens, (((0,), (1,)), ((), ())), preferred_element_type=F32)


def standardized(gate, up):
    hidden = jax.nn.silu(gate) * up
    mean = jnp.mean(hidden, axis=1, keepdims=True)
    centered = hidden - mean
    var = jnp.mean(centered * centered, axis=1, keepdims=True)
    return (centered * lax.rsqrt(var + 1e-05)).astype(BF)


def projected(weight, tokens, plan):
    depth, units = weight.shape
    count = tokens.shape[0]
    rows, wide = units // (Z * Y), 2 * TILE
    steps = units // wide

    def kernel(w_ref, t_ref, *refs):
        outs, total = refs[:-1], refs[-1]
        step = pl.program_id(0)
        at = pl.ds(pl.multiple_of(step * wide, wide), wide)
        total[at] = project(w_ref[...], t_ref[...])

        @pl.when(step == steps - 1)
        def _():
            outer = lax.axis_index("outer")
            y, z = outer % Y, outer // Y
            for n, place, dz, dy in plan["parts"]:
                row = pl.multiple_of(((z + dz) % Z * Y + (y + dy) % Y) * rows, BLOCK)
                part = total[pl.ds(row, rows)].astype(outs[n].dtype)
                if place is None:
                    outs[n][...] = part
                else:
                    outs[n][place] = part

    whole = lambda shape: pl.BlockSpec(shape, lambda i: (0,) * len(shape), pipeline_mode=pl.Buffered(1))
    shapes = [((*lead, rows, count), dtype) for lead, dtype in plan["shapes"]]
    return pl.pallas_call(
        kernel,
        grid=(steps,),
        in_specs=[pl.BlockSpec((depth, wide), lambda i: (0, i)), whole((count, depth))],
        out_specs=[whole(shape) for shape, _ in shapes],
        out_shape=[jax.ShapeDtypeStruct(shape, dtype) for shape, dtype in shapes],
        scratch_shapes=[pltpu.VMEM((units, count), F32)],
        compiler_params=pltpu.CompilerParams(vmem_limit_bytes=28 * 1024 * 1024),
        cost_estimate=pl.CostEstimate(flops=2 * depth * units * count, bytes_accessed=2 * depth * (units + count), transcendentals=0),
    )(in_hbm(weight), tokens)


STEPS_Y = (2, 1, 3)
GATE_PLAN = {
    "shapes": [((Z,), F32)] + [((Z,), BF)] * 3,
    "parts": [(n + 1, dz, dz, k) for n, k in enumerate(STEPS_Y) for dz in range(Z)] + [(0, dz, dz, 0) for dz in range(Z)],
}
UP_PLAN = {
    "shapes": [((Y,), F32)] + [((), BF)] * 4,
    "parts": [(n + 1, None, 1, k) for n, k in enumerate((2, 1, 3, 0))] + [(0, k, 0, k) for k in range(Y)],
}


def summed_y_first(weight, tokens):
    total, *parts = projected(weight, tokens, GATE_PLAN)
    came = [to_outer(part, along_y(k)) for k, part in zip(STEPS_Y, parts)]
    for c in came:
        total = total + c.astype(F32)
    narrow = total[1].astype(BF)
    other = to_outer(narrow, across_z())
    return total[0] + other.astype(F32)


def summed_z_first(weight, tokens):
    own, *parts = projected(weight, tokens, UP_PLAN)
    came = {k: to_outer(part, across_z()) for k, part in zip((2, 1, 3, 0), parts)}
    total, narrow = {}, {}
    for k in came:
        total[k] = own[k] + came[k].astype(F32)
        if k:
            narrow[k] = total[k].astype(BF)
            own, narrow[k] = lax.optimization_barrier((own, narrow[k]))
    result = total[0]
    for k in STEPS_Y:
        result = result + to_outer(narrow[k], along_y(k)).astype(F32)
    return result


def gathered(score):
    held = {0: score}
    for k in STEPS_Y:
        held[k] = to_outer(score, along_y(k))
    pieces = []
    for k in (0, *STEPS_Y):
        pieces += [(held[k], 0, k), (to_outer(held[k], across_z()), 1, k)]
    return pieces


def in_hbm(array):
    return pltpu.with_memory_space_constraint(array, pltpu.HBM)


def moved(kernel, shapes, n_copies, root, arrays):
    size = sum(2 * jnp.size(a) for a in (jax.eval_shape(lambda s=s: jnp.zeros(s, BF)) for s in shapes))
    return pl.pallas_call(
        kernel,
        in_specs=[pl.BlockSpec(memory_space=pltpu.SMEM)] + [pl.BlockSpec(memory_space=pl.ANY)] * len(arrays),
        out_specs=[pl.BlockSpec(memory_space=pltpu.VMEM)] * len(shapes),
        out_shape=[jax.ShapeDtypeStruct(s, BF) for s in shapes],
        scratch_shapes=[pltpu.SemaphoreType.DMA((n_copies,))],
        compiler_params=pltpu.CompilerParams(vmem_limit_bytes=16 * 1024 * 1024),
        cost_estimate=pl.CostEstimate(flops=0, bytes_accessed=2 * size, transcendentals=0),
    )(root[None], *arrays)


def halves(weights, root):
    depth, units = weights[0].shape
    half = units // 2

    def kernel(root_ref, *refs):
        ins, out, sems = refs[:2], refs[2], refs[3]
        at = pl.multiple_of((1 - lax.axis_index("inner") % 2) * half, TILE)
        copies = [pltpu.make_async_copy(ins[n].at[:, pl.ds(at, half)], out.at[n], sems.at[n]) for n in range(2)]
        for c in copies:
            c.start()
        for c in copies:
            c.wait()

    return moved(kernel, [(2, depth, half)], 2, root, weights)[0]


def chunks(weights, swapped, root):
    depth, units = weights[0].shape
    half, wide = units // 2, 2 * TILE

    def kernel(root_ref, *refs):
        ins, outs, sems = refs[:3], refs[3:-1], refs[-1]
        inner = lax.axis_index("inner")
        x, c = inner // 2 % X, inner % 2
        at_home = root_ref[0] % 2 == c
        copies = []
        for k in range(X):
            at = jnp.minimum((x + k) % X * wide, half - wide)
            for n in range(2):
                sem, out = sems.at[2 * k + n], outs[k].at[n]
                here = pltpu.make_async_copy(ins[n].at[:, pl.ds(pl.multiple_of(c * half + at, TILE), wide)], out, sem)
                there = pltpu.make_async_copy(ins[2].at[n, :, pl.ds(pl.multiple_of(at, TILE), wide)], out, sem)
                pl.when(at_home)(here.start)
                pl.when(jnp.logical_not(at_home))(there.start)
                copies.append(there)
        for made in copies:
            made.wait()

    return moved(kernel, [(2, depth, wide)] * X, 2 * X, root, (*weights, swapped))


def tiles(held, root):
    depth = held[0].shape[1]

    def kernel(root_ref, *refs):
        ins, outs, sems = refs[:X], refs[X:-1], refs[-1]
        inner = lax.axis_index("inner")
        h, x = inner // 8, inner // 2 % X
        away = (x + X - root_ref[0] // 2 % X) % X
        copies = []
        for n, which in enumerate((h, 1 - h)):
            for k in range(X):
                at = pl.ds(pl.multiple_of(which * TILE, TILE), TILE)
                made = pltpu.make_async_copy(ins[k].at[:, :, at], outs[n], sems.at[n])
                pl.when(away == k)(made.start)
            copies.append(made)
        for made in copies:
            made.wait()

    return moved(kernel, [(2, depth, TILE)] * 2, 2, root, held)


def slab_partials(mine, other, tokens, root):
    depth, count = mine.shape[1], tokens.shape[0]

    def kernel(root_ref, mine_ref, other_ref, t_ref, *refs):
        outs, total = refs[:-1], refs[-1]
        outer = lax.axis_index("outer")
        y, z = outer % Y, outer // Y
        at_home = root_ref[0] // 8 == lax.axis_index("inner") // 8
        for n in range(2):

            @pl.when(at_home)
            def _():
                total[n] = project(mine_ref[n], t_ref[...])

            @pl.when(jnp.logical_not(at_home))
            def _():
                total[n] = project(other_ref[n], t_ref[...])

            for k in range(Y):
                for dz in range(Z):
                    row = ((z + dz) % Z * Y + (y + k) % Y) * BLOCK
                    outs[k][n, dz] = total[n, pl.ds(pl.multiple_of(row, BLOCK), BLOCK)]

    vmem = pl.BlockSpec(memory_space=pltpu.VMEM)
    return pl.pallas_call(
        kernel,
        in_specs=[pl.BlockSpec(memory_space=pltpu.SMEM)] + [vmem] * 3,
        out_specs=[vmem] * Y,
        out_shape=[jax.ShapeDtypeStruct((2, Z, BLOCK, count), F32)] * Y,
        scratch_shapes=[pltpu.VMEM((2, TILE, count), F32)],
        compiler_params=pltpu.CompilerParams(vmem_limit_bytes=16 * 1024 * 1024),
        cost_estimate=pl.CostEstimate(flops=4 * depth * TILE * count, bytes_accessed=4 * count * depth, transcendentals=0),
    )(root[None], mine, other, tokens)


def spread(weights, tokens, root):
    weights = [in_hbm(w) for w in weights]
    half = halves(weights, root)
    swapped = to_inner(half, flip(1))
    chunk = chunks(weights, swapped, root)
    held = [chunk[0]] + [to_inner(chunk[k], along_x(k)) for k in (1, 2, 3)]
    mine, other = tiles(held, root)
    other = to_inner(other, flip(8))
    return slab_partials(mine, other, tokens, root)


def slab_moves():
    moves = []
    for i in range(16):
        h, x, c = i // 8, i // 2 % X, i % 2
        tile = min(2 * x, 5) + h
        if x == 3 and h == 0:
            continue
        for o in range(Z * Y):
            unit = 8 * (7 * c + tile) + o
            moves.append((o * 16 + i, unit // 14 * 16 + unit % 14))
    return moves


def correlate(pieces, blocks, rows, count):
    n_units = Z * Y * rows
    wide = 2 * TILE
    order = (0, 1, 8, 9)

    def kernel(*refs):
        ins, out, slab, scores, sems = refs[:-4], refs[-4], refs[-3], refs[-2], refs[-1]
        outer, inner = lax.axis_index("outer"), lax.axis_index("inner")
        z, y = outer // Y, outer % Y
        h, x, c = inner // 8, inner // 2 % X, inner % 2
        copies = []

        def copy(src, dst):
            made = pltpu.make_async_copy(src, dst, sems.at[len(copies)])
            made.start()
            copies.append(made)

        for ref, (_, dz, dy) in zip(ins, pieces):
            row = ((z + dz) % Z * Y + (y + Y - dy) % Y) * rows
            copy(ref, scores.at[pl.ds(pl.multiple_of(row, BLOCK), rows)])
        for ref, (block, dx) in zip(ins[len(pieces) :], blocks):
            for n, bits in enumerate(order):
                to_h, to_c = (h + bits // 8) % 2, (c + bits % 2) % 2
                slot = to_h * 8 + (x + X - dx) % X * 2 + to_c
                copy(ref.at[n], slab.at[pl.ds(pl.multiple_of(slot * BLOCK, BLOCK), BLOCK)])
        for made in copies:
            made.wait()
        left = slab[:rows]
        for n in range(n_units // wide):
            right = scores[n * wide : (n + 1) * wide]
            gram = lax.dot_general(left, right, (((1,), (1,)), ((), ())), preferred_element_type=F32)
            out[:, n * wide : (n + 1) * wide] = gram / count

    arrays = [p[0] for p in pieces] + [b[0] for b in blocks]
    n_copies = sum(a.shape[0] if a.ndim == 3 else 1 for a in arrays)
    return pl.pallas_call(
        kernel,
        out_shape=jax.ShapeDtypeStruct((rows, n_units), F32),
        in_specs=[pl.BlockSpec(memory_space=pl.ANY)] * len(arrays),
        out_specs=pl.BlockSpec(memory_space=pltpu.VMEM),
        scratch_shapes=[
            pltpu.VMEM((16 * BLOCK, count), BF),
            pltpu.VMEM((n_units, count), BF),
            pltpu.SemaphoreType.DMA((n_copies,)),
        ],
        compiler_params=pltpu.CompilerParams(vmem_limit_bytes=24 * 1024 * 1024),
        cost_estimate=pl.CostEstimate(
            flops=2 * rows * n_units * count, bytes_accessed=2 * (rows + n_units) * count + 4 * rows * n_units, transcendentals=0
        ),
    )(*arrays)


def local(tokens, base_gate, base_up, adjusted_gate, adjusted_up, slab_block):
    units = base_gate.shape[1]
    count = tokens.shape[0]
    rows = units // (Z * Y)
    root = slab_block[0]
    total, *parts = spread((base_gate, base_up), tokens, root)
    gate = summed_y_first(adjusted_gate, tokens)
    up = summed_z_first(adjusted_up, tokens)
    pieces = gathered(standardized(gate, up))

    for k, part in zip((1, 2, 3), parts):
        total = total + to_outer(part, along_y(k))
    total = total[:, 0] + to_outer(total[:, 1], across_z())
    score = standardized(total[0], total[1])
    score = lax.ppermute(score, ("outer", "inner"), slab_moves())
    two = jnp.stack([score, to_inner(score, flip(1))])
    four = jnp.concatenate([two, to_inner(two, flip(8))])
    blocks = [(four, 0)] + [(to_inner(four, along_x(k)), k) for k in (2, 1, 3)]
    return correlate(pieces, blocks, rows, count)


def solution(mesh):
    return jax.shard_map(
        local,
        mesh=mesh,
        in_specs=(
            P(None, "outer"),
            P("outer", "inner"),
            P("outer", "inner"),
            P("outer", "inner"),
            P("outer", "inner"),
            P(),
        ),
        out_specs=P("outer", "inner"),
        check_vma=False,
    )
```
